128 devices in a mesh: tm: 32 (over y, z, core), space: 4 (over x).
Axes of the slice: x: 4, y: 4, z: 4, core: 2. Of those that a mesh axis runs over, the one named last changes fastest.
Arguments:
- scenes: float32 [32, 4096, 2048], P('tm', None, 'space'), may hold values from -6 to 6
- offset_y: int32 [32], replicated, may hold values from -2048 to 2048
- offset_x: int32 [32], replicated, may hold values from -63 to 63
- frac_y: float32 [32], replicated, may hold values from 0.05 to 0.95
- frac_x: float32 [32], replicated, may hold values from 0.05 to 0.95
Outputs:
- warped: float32 [32, 4096, 2048], P(None, 'tm', 'space')
The draws below stay inside these ranges and needn't reach their ends.
All inputs are finite; a program needn't handle non-finite values.
Results may differ from the reference program's by a relative error of at most 0.0003.
Values sent between devices are 32-bit elements; how exact they have to be, the bound alone decides.
A program may use at most 128 MiB of HBM per device.

```python
import jax
import jax.numpy as jnp
from jax import lax

HALO = 64
ROWS = 4096
SCENES = 32
COLS = 2048


def place_ends(array, own_key, least, high):
    shape = array.shape
    place = [jax.random.randint(jax.random.fold_in(own_key, axis), (), 0, shape[axis]) for axis in range(len(shape))]
    array = array.at[tuple(place)].set(least)
    longest = shape.index(max(shape))
    place[longest] = (place[longest] + 1) % shape[longest]
    return array.at[tuple(place)].set(high)


def block_levels(stream_key, dims, split, smallest, high):
    factor_of, own = 1.0, jax.random.fold_in(stream_key, 6)
    for dim, blocks in split:
        steps = jnp.exp(jax.random.uniform(jax.random.fold_in(own, dim), (blocks,), jnp.float32, smallest / len(split), high / len(split)))
        factor_of = factor_of * jnp.repeat(steps, dims[dim] // blocks).reshape([-1 if axis == dim else 1 for axis in range(len(dims))])
    return factor_of


def bell_draw(key, extent, scale, reach, pieces=(), kind=jnp.bfloat16):
    gain = block_levels(key, extent, pieces, -0.22, 0.18) if pieces else 1.0
    values = jax.random.normal(key, extent, jnp.float32) * scale * gain
    return jnp.minimum(jnp.maximum(values, -reach), reach).astype(kind)


def setup_inputs(seed: int = 0) -> dict:
    key_of = jax.random.split(jax.random.key(seed), 6)
    scenes = bell_draw(key_of[0], (SCENES, ROWS, COLS), 1.0, 6.0, ((0, 32), (2, 4)), jnp.float32)
    offset_y = place_ends(jax.random.randint(key_of[1], (SCENES,), 0 - ROWS // 2, ROWS // 2 + 1), jax.random.fold_in(key_of[1], 1), 0 - ROWS // 2, (ROWS // 2 + 1) - 1).astype(jnp.int32)
    offset_x = place_ends(jax.random.randint(key_of[2], (SCENES,), 1 - HALO, HALO), jax.random.fold_in(key_of[2], 1), 1 - HALO, HALO - 1).astype(jnp.int32)
    frac_y = jnp.clip(jax.random.uniform(key_of[3], (SCENES,), jnp.float32, 0.05, 0.95), 0.05, 0.95)
    frac_x = jnp.clip(jax.random.uniform(key_of[4], (SCENES,), jnp.float32, 0.05, 0.95), 0.05, 0.95)
    return dict(scenes=scenes, offset_y=offset_y, offset_x=offset_x, frac_y=frac_y, frac_x=frac_x)


def reference(scenes, offset_y, offset_x, frac_y, frac_x):
    grid_rows = scenes.shape[1]
    grid_cols = scenes.shape[2]
    pad_rows = grid_rows // 2 + 2
    pad_cols = HALO + 2

    def resample(inputs):
        image, offset_row, offset_col, weight_row, weight_col = inputs
        padded = jnp.pad(image, ((pad_rows, pad_rows), (pad_cols, pad_cols)))

        def shifted(lag_row, lag_col):
            start_row = (pad_rows - offset_row - lag_row).astype(jnp.int32)
            start_col = (pad_cols - offset_col - lag_col).astype(jnp.int32)
            return lax.dynamic_slice(padded, (start_row, start_col), (grid_rows, grid_cols))

        result = weight_row * weight_col * shifted(1, 1)
        result = result + weight_row * (1.0 - weight_col) * shifted(1, 0)
        result = result + (1.0 - weight_row) * weight_col * shifted(0, 1)
        result = result + (1.0 - weight_row) * (1.0 - weight_col) * shifted(0, 0)
        return result

    return lax.map(resample, (scenes, offset_y, offset_x, frac_y, frac_x))
```

```python
import jax
import jax.numpy as jnp
from jax import lax
from jax.experimental import pallas as pl
from jax.experimental.pallas import tpu as pltpu
from jax.sharding import PartitionSpec as P

MESH = pl.DeviceIdType.MESH
LANES = 128
PAD = 136
PIECE = 32


def send_order():
    groups = (
        ((1, 0), (3, 0), (0, 1), (0, 3)),
        ((1, 1), (3, 3)),
        ((1, 3), (3, 1)),
        ((2, 0), (0, 2)),
        ((2, 1), (1, 2), (2, 3), (3, 2)),
        ((2, 2),),
    )
    order = [(dy, dz, dc) for group in groups for dc in range(2) for dy, dz in group]
    return order + [(0, 0, 1)]


ORDER = send_order()


def warp_kernel(
    oy_ref, ox_ref, fy_ref, fx_ref, scene_ref, out_ref,
    src, send, pack_out, pack_in, load_sem, send_sem, recv_sem, halo_send_sem, halo_recv_sem,
):
    rows = scene_ref.shape[1]
    tiles = scene_ref.shape[2] // LANES
    tile_rows = out_ref.shape[1]
    half = rows // 2
    me = lax.axis_index("tm")
    x = lax.axis_index("space")
    y, z, core = me // 8, (me // 2) % 4, me % 2

    def member(dy, dz, dc, sign):
        return (
            ((y + sign * dy + 4) % 4) * 8 + ((z + sign * dz + 4) % 4) * 2 + (core + dc) % 2
        )

    left, right = (x + 3) % 4, (x + 1) % 4

    barrier = pltpu.get_barrier_semaphore()
    for dy, dz, dc in ORDER:
        pl.semaphore_signal(
            barrier, inc=1, device_id=(member(dy, dz, dc, -1), x), device_id_type=MESH
        )
    for side in (left, right):
        pl.semaphore_signal(barrier, inc=1, device_id=(me, side), device_id_type=MESH)

    loads = []
    for tile in range(tiles):
        load = pltpu.make_async_copy(
            scene_ref.at[0, :, pl.ds(tile * LANES, LANES)],
            src.at[tile, pl.ds(PAD, rows)],
            load_sem.at[tile],
        )
        load.start()
        loads.append(load)
    zero_rows = jnp.zeros((PAD, LANES), jnp.float32)
    for plane in range(tiles + 1):
        src[plane, pl.ds(0, PAD)] = zero_rows
        src[plane, pl.ds(PAD + rows, PAD)] = zero_rows

    shift_y, shift_x = oy_ref[me], ox_ref[me]
    weight_y, weight_x = fy_ref[me], fx_ref[me]
    lane = lax.broadcasted_iota(jnp.int32, (PIECE, LANES), 1)
    rightward = shift_x >= 0
    low = jnp.where(rightward, 0, -shift_x)
    high = jnp.where(rightward, LANES - shift_x, LANES)
    low_before = jnp.where(rightward, 0, -shift_x - 1)
    high_before = jnp.where(rightward, LANES - 1 - shift_x, LANES)
    own_at = (lane >= low) & (lane < high)
    own_before = (lane >= low_before) & (lane < high_before)
    roll_at = (shift_x + LANES) % LANES
    roll_before = (shift_x + 1 + LANES) % LANES
    step = jnp.where(rightward, tiles, 1)

    def blend(dest, tile, part):
        base = jnp.clip(dest * tile_rows - shift_y - 1, -tile_rows - 1, rows)
        base = base + (PAD + part * PIECE)

        def blend_rows(plane):
            above = src[plane, pl.ds(base, PIECE)]
            at = src[plane, pl.ds(base + 1, PIECE)]
            return weight_y * above + (1.0 - weight_y) * at

        own = blend_rows(tile)
        beside = blend_rows((tile + step) % (tiles + 1))
        at = pltpu.roll(jnp.where(own_at, own, beside), roll_at, 1)
        before = pltpu.roll(jnp.where(own_before, own, beside), roll_before, 1)
        return weight_x * before + (1.0 - weight_x) * at

    parts = tile_rows // PIECE

    def send_piece(tile, part):
        lanes = pl.ds(pl.multiple_of(tile * LANES, LANES), LANES)
        piece = pl.ds(pl.multiple_of(part * PIECE, PIECE), PIECE)
        for slot, (dy, dz, dc) in enumerate(ORDER):
            dest = member(dy, dz, dc, 1)
            send[slot, tile, piece] = blend(dest, tile, part)
            pltpu.make_async_remote_copy(
                src_ref=send.at[slot, tile, piece],
                dst_ref=out_ref.at[me, piece, lanes],
                send_sem=send_sem.at[slot],
                recv_sem=recv_sem.at[slot],
                device_id=(dest, x),
                device_id_type=MESH,
            ).start()

    for load in loads:
        load.wait()
    pl.semaphore_wait(barrier, len(ORDER) + 2)

    lower = lax.broadcasted_iota(jnp.int32, (64, LANES), 1) < LANES // 2

    def pack(index, carry):
        top = pl.ds(pl.multiple_of(PAD + index * 64, 8), 64)
        bottom = pl.ds(pl.multiple_of(PAD + half + index * 64, 8), 64)
        packed = pl.ds(pl.multiple_of(index * 64, 64), 64)
        first, last = src[0, bottom], src[tiles - 1, bottom]
        pack_out[0, packed] = jnp.where(lower, src[0, top], pltpu.roll(first, LANES // 2, 1))
        pack_out[1, packed] = jnp.where(lower, pltpu.roll(last, LANES // 2, 1), src[tiles - 1, top])
        return carry

    lax.fori_loop(0, half // 64, pack, 0)
    halos = []
    for side, target in enumerate((left, right)):
        halo = pltpu.make_async_remote_copy(
            src_ref=pack_out.at[side],
            dst_ref=pack_in.at[side],
            send_sem=halo_send_sem.at[side],
            recv_sem=halo_recv_sem.at[side],
            device_id=(me, target),
            device_id_type=MESH,
        )
        halo.start()
        halos.append(halo)

    def inner(index, carry):
        send_piece(1 + index // parts, index % parts)
        return carry

    lax.fori_loop(0, 2 * parts, inner, 0)

    for halo in halos:
        halo.wait()

    has_left = x > 0
    has_right = x < 3

    def unpack(index, carry):
        top = pl.ds(pl.multiple_of(PAD + index * 64, 8), 64)
        bottom = pl.ds(pl.multiple_of(PAD + half + index * 64, 8), 64)
        packed = pl.ds(pl.multiple_of(index * 64, 64), 64)
        from_right = jnp.where(has_right, pack_in[0, packed], 0.0)
        from_left = jnp.where(has_left, pack_in[1, packed], 0.0)
        src[tiles, top] = jnp.where(lower, from_right, from_left)
        src[tiles, bottom] = pltpu.roll(jnp.where(lower, from_left, from_right), LANES // 2, 1)
        return carry

    lax.fori_loop(0, half // 64, unpack, 0)

    def outer(index, carry):
        send_piece((tiles - 1) * (index // parts), index % parts)
        return carry

    lax.fori_loop(0, 2 * parts, outer, 0)

    def keep(index, carry):
        for tile in range(tiles):
            piece = pl.ds(pl.multiple_of(index * PIECE, PIECE), PIECE)
            out_ref[me, piece, pl.ds(tile * LANES, LANES)] = blend(me, tile, index)
        return carry

    lax.fori_loop(0, parts, keep, 0)

    for slot, (dy, dz, dc) in enumerate(ORDER):
        source = member(dy, dz, dc, -1)
        pltpu.make_async_copy(send.at[slot], send.at[slot], send_sem.at[slot]).wait()
        pltpu.make_async_copy(out_ref.at[source], out_ref.at[source], recv_sem.at[slot]).wait()


def body(scenes, offset_y, offset_x, frac_y, frac_x):
    rows, cols = scenes.shape[1:]
    tiles = cols // LANES
    members = lax.axis_size("tm")
    tile_rows = rows // members
    smem = pl.BlockSpec(memory_space=pltpu.SMEM)
    return pl.pallas_call(
        warp_kernel,
        out_shape=jax.ShapeDtypeStruct((members, tile_rows, cols), jnp.float32),
        in_specs=[smem, smem, smem, smem, pl.BlockSpec(memory_space=pltpu.HBM)],
        out_specs=pl.BlockSpec(memory_space=pltpu.VMEM),
        scratch_shapes=[
            pltpu.VMEM((tiles + 1, rows + 2 * PAD, LANES), jnp.float32),
            pltpu.VMEM((len(ORDER), tiles, tile_rows, LANES), jnp.float32),
            pltpu.VMEM((2, rows // 2, LANES), jnp.float32),
            pltpu.VMEM((2, rows // 2, LANES), jnp.float32),
            pltpu.SemaphoreType.DMA((tiles,)),
            pltpu.SemaphoreType.DMA((len(ORDER),)),
            pltpu.SemaphoreType.DMA((len(ORDER),)),
            pltpu.SemaphoreType.DMA((2,)),
            pltpu.SemaphoreType.DMA((2,)),
        ],
        compiler_params=pltpu.CompilerParams(
            collective_id=0, has_side_effects=True, vmem_limit_bytes=48 << 20
        ),
    )(offset_y, offset_x, frac_y, frac_x, scenes)


def solution(mesh):
    return jax.shard_map(
        body,
        mesh=mesh,
        in_specs=(P("tm", None, "space"), P(), P(), P(), P()),
        out_specs=P(None, "tm", "space"),
        check_vma=False,
    )
```

```python
import jax
import jax.numpy as jnp
from jax import lax
from jax.experimental import pallas as pl
from jax.experimental.pallas import tpu as pltpu
from jax.sharding import PartitionSpec as P

MESH = pl.DeviceIdType.MESH
LANES = 128
PAD = 136
PIECE = 64


def send_order():
    groups = (
        ((1, 0), (3, 0), (0, 1), (0, 3)),
        ((1, 1), (3, 3)),
        ((1, 3), (3, 1)),
        ((2, 0), (0, 2)),
        ((2, 1), (1, 2), (2, 3), (3, 2)),
        ((2, 2),),
    )
    order = [(dy, dz, dc) for group in groups for dc in range(2) for dy, dz in group]
    return order + [(0, 0, 1)]


ORDER = send_order()


def warp_kernel(
    oy_hbm, ox_hbm, fy_hbm, fx_hbm, scene_ref, out_ref,
    oy_ref, ox_ref, fy_ref, fx_ref, src, send, pack_out, pack_in,
    load_sem, param_sem, send_sem, recv_sem, halo_send_sem, halo_recv_sem,
):
    rows = scene_ref.shape[1]
    tiles = scene_ref.shape[2] // LANES
    tile_rows = out_ref.shape[1]
    half = rows // 2
    me = lax.axis_index("tm")
    x = lax.axis_index("space")
    y, z, core = me // 8, (me // 2) % 4, me % 2

    def member(dy, dz, dc, sign):
        return (
            ((y + sign * dy + 4) % 4) * 8 + ((z + sign * dz + 4) % 4) * 2 + (core + dc) % 2
        )

    left, right = (x + 3) % 4, (x + 1) % 4

    barrier = pltpu.get_barrier_semaphore()
    for dy, dz, dc in ORDER:
        pl.semaphore_signal(
            barrier, inc=1, device_id=(member(dy, dz, dc, -1), x), device_id_type=MESH
        )
    for side in (left, right):
        pl.semaphore_signal(barrier, inc=1, device_id=(me, side), device_id_type=MESH)

    loads = []
    params = ((oy_hbm, oy_ref), (ox_hbm, ox_ref), (fy_hbm, fy_ref), (fx_hbm, fx_ref))
    for index, (hbm, smem) in enumerate(params):
        load = pltpu.make_async_copy(hbm, smem, param_sem.at[index])
        load.start()
        loads.append(load)
    for tile in range(tiles):
        load = pltpu.make_async_copy(
            scene_ref.at[0, :, pl.ds(tile * LANES, LANES)],
            src.at[tile, pl.ds(PAD, rows)],
            load_sem.at[tile],
        )
        load.start()
        loads.append(load)
    zero_rows = jnp.zeros((PAD, LANES), jnp.float32)
    for plane in range(tiles + 1):
        src[plane, pl.ds(0, PAD)] = zero_rows
        src[plane, pl.ds(PAD + rows, PAD)] = zero_rows

    for load in loads:
        load.wait()

    shift_y, shift_x = oy_ref[me], ox_ref[me]
    weight_y, weight_x = fy_ref[me], fx_ref[me]
    lane = lax.broadcasted_iota(jnp.int32, (PIECE, LANES), 1)
    rightward = shift_x >= 0
    low = jnp.where(rightward, 0, -shift_x)
    high = jnp.where(rightward, LANES - shift_x, LANES)
    low_before = jnp.where(rightward, 0, -shift_x - 1)
    high_before = jnp.where(rightward, LANES - 1 - shift_x, LANES)
    own_at = (lane >= low) & (lane < high)
    own_before = (lane >= low_before) & (lane < high_before)
    roll_at = (shift_x + LANES) % LANES
    roll_before = (shift_x + 1 + LANES) % LANES
    step = jnp.where(rightward, tiles, 1)

    def blend(dest, tile, part):
        base = jnp.clip(dest * tile_rows - shift_y - 1, -tile_rows - 1, rows)
        base = base + (PAD + part * PIECE)

        def blend_rows(plane):
            above = src[plane, pl.ds(base, PIECE)]
            at = src[plane, pl.ds(base + 1, PIECE)]
            return weight_y * above + (1.0 - weight_y) * at

        own = blend_rows(tile)
        beside = blend_rows((tile + step) % (tiles + 1))
        at = pltpu.roll(jnp.where(own_at, own, beside), roll_at, 1)
        before = pltpu.roll(jnp.where(own_before, own, beside), roll_before, 1)
        return weight_x * before + (1.0 - weight_x) * at

    parts = tile_rows // PIECE

    def send_piece(tile, part):
        lanes = pl.ds(pl.multiple_of(tile * LANES, LANES), LANES)
        piece = pl.ds(pl.multiple_of(part * PIECE, PIECE), PIECE)
        for slot, (dy, dz, dc) in enumerate(ORDER):
            dest = member(dy, dz, dc, 1)
            send[slot, tile, piece] = blend(dest, tile, part)
            pltpu.make_async_remote_copy(
                src_ref=send.at[slot, tile, piece],
                dst_ref=out_ref.at[me, piece, lanes],
                send_sem=send_sem.at[slot],
                recv_sem=recv_sem.at[slot],
                device_id=(dest, x),
                device_id_type=MESH,
            ).start()

    pl.semaphore_wait(barrier, len(ORDER) + 2)

    lower = lax.broadcasted_iota(jnp.int32, (64, LANES), 1) < LANES // 2

    def pack(index, carry):
        top = pl.ds(pl.multiple_of(PAD + index * 64, 8), 64)
        bottom = pl.ds(pl.multiple_of(PAD + half + index * 64, 8), 64)
        packed = pl.ds(pl.multiple_of(index * 64, 64), 64)
        first, last = src[0, bottom], src[tiles - 1, bottom]
        pack_out[0, packed] = jnp.where(lower, src[0, top], pltpu.roll(first, LANES // 2, 1))
        pack_out[1, packed] = jnp.where(lower, pltpu.roll(last, LANES // 2, 1), src[tiles - 1, top])
        return carry

    halos = [
        pltpu.make_async_remote_copy(
            src_ref=pack_out.at[side],
            dst_ref=pack_in.at[side],
            send_sem=halo_send_sem.at[side],
            recv_sem=halo_recv_sem.at[side],
            device_id=(me, target),
            device_id_type=MESH,
        )
        for side, target in enumerate((left, right))
    ]

    def inner(index, carry):
        send_piece(1 + index // parts, index % parts)

        @pl.when(index == 0)
        def _():
            lax.fori_loop(0, half // 64, pack, 0)
            for halo in halos:
                halo.start()

        return carry

    lax.fori_loop(0, 2 * parts, inner, 0)

    for halo in halos:
        halo.wait()

    has_left = x > 0
    has_right = x < 3

    def unpack(index, carry):
        top = pl.ds(pl.multiple_of(PAD + index * 64, 8), 64)
        bottom = pl.ds(pl.multiple_of(PAD + half + index * 64, 8), 64)
        packed = pl.ds(pl.multiple_of(index * 64, 64), 64)
        from_right = jnp.where(has_right, pack_in[0, packed], 0.0)
        from_left = jnp.where(has_left, pack_in[1, packed], 0.0)
        src[tiles, top] = jnp.where(lower, from_right, from_left)
        src[tiles, bottom] = pltpu.roll(jnp.where(lower, from_left, from_right), LANES // 2, 1)
        return carry

    lax.fori_loop(0, half // 64, unpack, 0)

    def outer(index, carry):
        send_piece((tiles - 1) * (index // parts), index % parts)
        return carry

    lax.fori_loop(0, 2 * parts, outer, 0)

    def keep(index, carry):
        for tile in range(tiles):
            piece = pl.ds(pl.multiple_of(index * PIECE, PIECE), PIECE)
            out_ref[me, piece, pl.ds(tile * LANES, LANES)] = blend(me, tile, index)
        return carry

    lax.fori_loop(0, parts, keep, 0)

    for slot, (dy, dz, dc) in enumerate(ORDER):
        source = member(dy, dz, dc, -1)
        pltpu.make_async_copy(send.at[slot], send.at[slot], send_sem.at[slot]).wait()
        pltpu.make_async_copy(out_ref.at[source], out_ref.at[source], recv_sem.at[slot]).wait()


def body(scenes, offset_y, offset_x, frac_y, frac_x):
    rows, cols = scenes.shape[1:]
    tiles = cols // LANES
    members = lax.axis_size("tm")
    tile_rows = rows // members
    return pl.pallas_call(
        warp_kernel,
        out_shape=jax.ShapeDtypeStruct((members, tile_rows, cols), jnp.float32),
        in_specs=[pl.BlockSpec(memory_space=pltpu.HBM)] * 5,
        out_specs=pl.BlockSpec(memory_space=pltpu.VMEM),
        scratch_shapes=[
            pltpu.SMEM(offset_y.shape, jnp.int32),
            pltpu.SMEM(offset_x.shape, jnp.int32),
            pltpu.SMEM(frac_y.shape, jnp.float32),
            pltpu.SMEM(frac_x.shape, jnp.float32),
            pltpu.VMEM((tiles + 1, rows + 2 * PAD, LANES), jnp.float32),
            pltpu.VMEM((len(ORDER), tiles, tile_rows, LANES), jnp.float32),
            pltpu.VMEM((2, rows // 2, LANES), jnp.float32),
            pltpu.VMEM((2, rows // 2, LANES), jnp.float32),
            pltpu.SemaphoreType.DMA((tiles,)),
            pltpu.SemaphoreType.DMA((4,)),
            pltpu.SemaphoreType.DMA((len(ORDER),)),
            pltpu.SemaphoreType.DMA((len(ORDER),)),
            pltpu.SemaphoreType.DMA((2,)),
            pltpu.SemaphoreType.DMA((2,)),
        ],
        compiler_params=pltpu.CompilerParams(
            collective_id=0, has_side_effects=True, vmem_limit_bytes=28 << 20
        ),
    )(*[pltpu.with_memory_space_constraint(v, pltpu.HBM) for v in (offset_y, offset_x, frac_y, frac_x, scenes)])


def solution(mesh):
    return jax.shard_map(
        body,
        mesh=mesh,
        in_specs=(P("tm", None, "space"), P(), P(), P(), P()),
        out_specs=P(None, "tm", "space"),
        check_vma=False,
    )
```

```python
import jax
import jax.numpy as jnp
from jax import lax
from jax.experimental import pallas as pl
from jax.experimental.pallas import tpu as pltpu
from jax.sharding import PartitionSpec as P

MESH = pl.DeviceIdType.MESH
LANES = 128
PAD = 136
PIECE = 64


NEAR = ((1, 0), (3, 0), (0, 1), (0, 3))
FAR = (
    (2, 2), (2, 1), (1, 2), (2, 3), (3, 2), (2, 0), (0, 2), (1, 1), (3, 3), (1, 3), (3, 1),
)
CHIPS = NEAR + FAR
PEERS = 2 * len(CHIPS) + 1


def warp_kernel(
    oy_hbm, ox_hbm, fy_hbm, fx_hbm, scene_ref, out_ref,
    oy_ref, ox_ref, fy_ref, fx_ref, first, last, send, pack_out, pack_in,
    load_sem, param_sem, send_sem, recv_sem, halo_send_sem, halo_recv_sem,
):
    rows = scene_ref.shape[1]
    tiles = scene_ref.shape[2] // LANES
    tile_rows = out_ref.shape[1]
    half = rows // 2
    me = lax.axis_index("tm")
    x = lax.axis_index("space")
    y, z, core = me // 8, (me // 2) % 4, me % 2

    def member(chip, other, sign):
        dy, dz = chip
        return ((y + sign * dy + 4) % 4) * 8 + ((z + sign * dz + 4) % 4) * 2 + (core + other) % 2

    left, right = (x + 3) % 4, (x + 1) % 4
    here = (0, 0)

    planes = [first.at[0], first.at[1], first.at[2], last.at[0], last.at[1]]
    params = ((oy_hbm, oy_ref), (ox_hbm, ox_ref), (fy_hbm, fy_ref), (fx_hbm, fx_ref))
    loads = []
    for index, (hbm, smem) in enumerate(params):
        load = pltpu.make_async_copy(hbm, smem, param_sem.at[index])
        load.start()
        loads.append(load)
    for tile in range(tiles):
        load = pltpu.make_async_copy(
            scene_ref.at[0, :, pl.ds(tile * LANES, LANES)],
            planes[tile].at[pl.ds(PAD, rows)],
            load_sem.at[tile],
        )
        load.start()
        loads.append(load)

    barrier = pltpu.get_barrier_semaphore()
    for chip in FAR + NEAR:
        for other in range(2):
            pl.semaphore_signal(
                barrier, inc=1, device_id=(member(chip, other, -1), x), device_id_type=MESH
            )
    pl.semaphore_signal(barrier, inc=1, device_id=(member(here, 1, -1), x), device_id_type=MESH)
    for side in (left, right):
        pl.semaphore_signal(barrier, inc=1, device_id=(me, side), device_id_type=MESH)

    zero_rows = jnp.zeros((PAD, LANES), jnp.float32)
    for plane in planes:
        plane[pl.ds(0, PAD)] = zero_rows
        plane[pl.ds(PAD + rows, PAD)] = zero_rows

    for load in loads[:-1]:
        load.wait()

    shift_y, shift_x = oy_ref[me], ox_ref[me]
    weight_y, weight_x = fy_ref[me], fx_ref[me]
    lane = lax.broadcasted_iota(jnp.int32, (PIECE, LANES), 1)
    rightward = shift_x >= 0
    low = jnp.where(rightward, 0, -shift_x)
    high = jnp.where(rightward, LANES - shift_x, LANES)
    low_before = jnp.where(rightward, 0, -shift_x - 1)
    high_before = jnp.where(rightward, LANES - 1 - shift_x, LANES)
    own_at = (lane >= low) & (lane < high)
    own_before = (lane >= low_before) & (lane < high_before)
    roll_at = (shift_x + LANES) % LANES
    roll_before = (shift_x + 1 + LANES) % LANES

    def blend(dest, tile, part):
        base = jnp.clip(dest * tile_rows - shift_y - 1, -tile_rows - 1, rows)
        base = base + (PAD + part * PIECE)

        def blend_rows(read):
            above = read(pl.ds(base, PIECE))
            at = read(pl.ds(base + 1, PIECE))
            return weight_y * above + (1.0 - weight_y) * at

        own = blend_rows(lambda at: planes[tile][at])
        if tile == 1:
            side = jnp.where(rightward, 0, 2)
            beside = blend_rows(lambda at: first[side, at])
        else:
            before, after = planes[(tile - 1) % (tiles + 1)], planes[tile + 1]
            beside = blend_rows(lambda at: jnp.where(rightward, before[at], after[at]))
        at = pltpu.roll(jnp.where(own_at, own, beside), roll_at, 1)
        before = pltpu.roll(jnp.where(own_before, own, beside), roll_before, 1)
        return weight_x * before + (1.0 - weight_x) * at

    parts = tile_rows // PIECE

    def send_piece(slot, dest, tile, part):
        piece = pl.ds(pl.multiple_of(part * PIECE, PIECE), PIECE)
        send[slot, tile, piece] = blend(dest, tile, part)
        pltpu.make_async_remote_copy(
            src_ref=send.at[slot, tile, piece],
            dst_ref=out_ref.at[me, piece, pl.ds(tile * LANES, LANES)],
            send_sem=send_sem.at[slot],
            recv_sem=recv_sem.at[slot],
            device_id=(dest, x),
            device_id_type=MESH,
        ).start()

    def send_tile(chips, tile):
        def step(index, carry):
            part, other = index // 2, index % 2
            for chip in chips:
                slot = 2 * CHIPS.index(chip) + other
                send_piece(slot, member(chip, other, 1), tile, part)
            return carry

        lax.fori_loop(0, 2 * parts, step, 0)

    pl.semaphore_wait(barrier, PEERS + 2)

    send_tile(NEAR, 1)
    loads[-1].wait()

    lower = lax.broadcasted_iota(jnp.int32, (64, LANES), 1) < LANES // 2

    def pack(index, carry):
        top = pl.ds(pl.multiple_of(PAD + index * 64, 8), 64)
        bottom = pl.ds(pl.multiple_of(PAD + half + index * 64, 8), 64)
        packed = pl.ds(pl.multiple_of(index * 64, 64), 64)
        low_edge, high_edge = planes[0], planes[tiles - 1]
        pack_out[0, packed] = jnp.where(
            lower, low_edge[top], pltpu.roll(low_edge[bottom], LANES // 2, 1)
        )
        pack_out[1, packed] = jnp.where(
            lower, pltpu.roll(high_edge[bottom], LANES // 2, 1), high_edge[top]
        )
        return carry

    halos = [
        pltpu.make_async_remote_copy(
            src_ref=pack_out.at[side],
            dst_ref=pack_in.at[side],
            send_sem=halo_send_sem.at[side],
            recv_sem=halo_recv_sem.at[side],
            device_id=(me, target),
            device_id_type=MESH,
        )
        for side, target in enumerate((left, right))
    ]

    send_tile(FAR, 1)
    lax.fori_loop(0, half // 64, pack, 0)
    for halo in halos:
        halo.start()

    send_tile(CHIPS, 2)

    for halo in halos:
        halo.wait()

    has_left = x > 0
    has_right = x < 3

    def unpack(index, carry):
        top = pl.ds(pl.multiple_of(PAD + index * 64, 8), 64)
        bottom = pl.ds(pl.multiple_of(PAD + half + index * 64, 8), 64)
        packed = pl.ds(pl.multiple_of(index * 64, 64), 64)
        from_right = jnp.where(has_right, pack_in[0, packed], 0.0)
        from_left = jnp.where(has_left, pack_in[1, packed], 0.0)
        planes[tiles][top] = jnp.where(lower, from_right, from_left)
        planes[tiles][bottom] = pltpu.roll(jnp.where(lower, from_left, from_right), LANES // 2, 1)
        return carry

    lax.fori_loop(0, half // 64, unpack, 0)

    send_tile(CHIPS, 0)
    send_tile(FAR, 3)

    def across(part, carry):
        for tile in range(tiles):
            send_piece(PEERS - 1, member(here, 1, 1), tile, part)
        return carry

    lax.fori_loop(0, parts, across, 0)

    for tile in (3,):
        send_tile(NEAR, tile)

    def keep(part, carry):
        for tile in range(tiles):
            piece = pl.ds(pl.multiple_of(part * PIECE, PIECE), PIECE)
            out_ref[me, piece, pl.ds(tile * LANES, LANES)] = blend(me, tile, part)
        return carry

    lax.fori_loop(0, parts, keep, 0)

    for slot in range(PEERS):
        chip, other = (here, 1) if slot == PEERS - 1 else (CHIPS[slot // 2], slot % 2)
        source = member(chip, other, -1)
        pltpu.make_async_copy(send.at[slot], send.at[slot], send_sem.at[slot]).wait()
        pltpu.make_async_copy(out_ref.at[source], out_ref.at[source], recv_sem.at[slot]).wait()


def body(scenes, offset_y, offset_x, frac_y, frac_x):
    rows, cols = scenes.shape[1:]
    tiles = cols // LANES
    members = lax.axis_size("tm")
    tile_rows = rows // members
    return pl.pallas_call(
        warp_kernel,
        out_shape=jax.ShapeDtypeStruct((members, tile_rows, cols), jnp.float32),
        in_specs=[pl.BlockSpec(memory_space=pltpu.HBM)] * 5,
        out_specs=pl.BlockSpec(memory_space=pltpu.VMEM),
        scratch_shapes=[
            pltpu.SMEM(offset_y.shape, jnp.int32),
            pltpu.SMEM(offset_x.shape, jnp.int32),
            pltpu.SMEM(frac_y.shape, jnp.float32),
            pltpu.SMEM(frac_x.shape, jnp.float32),
            pltpu.VMEM((3, rows + 2 * PAD, LANES), jnp.float32),
            pltpu.VMEM((2, rows + 2 * PAD, LANES), jnp.float32),
            pltpu.VMEM((PEERS, tiles, tile_rows, LANES), jnp.float32),
            pltpu.VMEM((2, rows // 2, LANES), jnp.float32),
            pltpu.VMEM((2, rows // 2, LANES), jnp.float32),
            pltpu.SemaphoreType.DMA((tiles,)),
            pltpu.SemaphoreType.DMA((4,)),
            pltpu.SemaphoreType.DMA((PEERS,)),
            pltpu.SemaphoreType.DMA((PEERS,)),
            pltpu.SemaphoreType.DMA((2,)),
            pltpu.SemaphoreType.DMA((2,)),
        ],
        compiler_params=pltpu.CompilerParams(
            collective_id=0, has_side_effects=True, vmem_limit_bytes=28 << 20
        ),
    )(*[pltpu.with_memory_space_constraint(v, pltpu.HBM) for v in (offset_y, offset_x, frac_y, frac_x, scenes)])


def solution(mesh):
    return jax.shard_map(
        body,
        mesh=mesh,
        in_specs=(P("tm", None, "space"), P(), P(), P(), P()),
        out_specs=P(None, "tm", "space"),
        check_vma=False,
    )
```

```python
import jax
import jax.numpy as jnp
from jax import lax
from jax.experimental import pallas as pl
from jax.experimental.pallas import tpu as pltpu
from jax.sharding import PartitionSpec as P

MESH = pl.DeviceIdType.MESH
LANES = 128
PAD = 136
PIECE = 64


NEAR = ((1, 0), (3, 0), (0, 1), (0, 3))
FAR = (
    (2, 2), (2, 1), (1, 2), (2, 3), (3, 2), (2, 0), (0, 2), (1, 1), (3, 3), (1, 3), (3, 1),
)
CHIPS = NEAR + FAR
PEERS = 2 * len(CHIPS) + 1


def warp_kernel(
    oy_hbm, ox_hbm, fy_hbm, fx_hbm, scene_ref, out_ref,
    oy_ref, ox_ref, fy_ref, fx_ref, first, last, send, pack_out, pack_in,
    load_sem, param_sem, send_sem, recv_sem, halo_send_sem, halo_recv_sem,
):
    rows = scene_ref.shape[1]
    tiles = scene_ref.shape[2] // LANES
    tile_rows = out_ref.shape[1]
    half = rows // 2
    me = lax.axis_index("tm")
    x = lax.axis_index("space")
    y, z, core = me // 8, (me // 2) % 4, me % 2

    def member(chip, other, sign):
        dy, dz = chip
        return ((y + sign * dy + 4) % 4) * 8 + ((z + sign * dz + 4) % 4) * 2 + (core + other) % 2

    left, right = (x + 3) % 4, (x + 1) % 4
    here = (0, 0)

    planes = [first.at[0], first.at[1], first.at[2], last.at[0], last.at[1]]
    params = ((oy_hbm, oy_ref), (ox_hbm, ox_ref), (fy_hbm, fy_ref), (fx_hbm, fx_ref))
    loads = []
    for index, (hbm, smem) in enumerate(params):
        load = pltpu.make_async_copy(hbm, smem, param_sem.at[index])
        load.start()
        loads.append(load)
    for tile in range(tiles):
        load = pltpu.make_async_copy(
            scene_ref.at[0, :, pl.ds(tile * LANES, LANES)],
            planes[tile].at[pl.ds(PAD, rows)],
            load_sem.at[tile],
        )
        load.start()
        loads.append(load)

    barrier = pltpu.get_barrier_semaphore()
    for chip in FAR + NEAR:
        for other in range(2):
            pl.semaphore_signal(
                barrier, inc=1, device_id=(member(chip, other, -1), x), device_id_type=MESH
            )
    pl.semaphore_signal(barrier, inc=1, device_id=(member(here, 1, -1), x), device_id_type=MESH)
    for side in (left, right):
        pl.semaphore_signal(barrier, inc=1, device_id=(me, side), device_id_type=MESH)

    zero_rows = jnp.zeros((PAD, LANES), jnp.float32)
    for plane in planes:
        plane[pl.ds(0, PAD)] = zero_rows
        plane[pl.ds(PAD + rows, PAD)] = zero_rows

    for load in loads[:-1]:
        load.wait()

    shift_y, shift_x = oy_ref[me], ox_ref[me]
    weight_y, weight_x = fy_ref[me], fx_ref[me]
    lane = lax.broadcasted_iota(jnp.int32, (PIECE, LANES), 1)
    rightward = shift_x >= 0
    low = jnp.where(rightward, 0, -shift_x)
    high = jnp.where(rightward, LANES - shift_x, LANES)
    low_before = jnp.where(rightward, 0, -shift_x - 1)
    high_before = jnp.where(rightward, LANES - 1 - shift_x, LANES)
    own_at = (lane >= low) & (lane < high)
    own_before = (lane >= low_before) & (lane < high_before)
    roll_at = (shift_x + LANES) % LANES
    roll_before = (shift_x + 1 + LANES) % LANES

    def blend(dest, tile, part):
        base = jnp.clip(dest * tile_rows - shift_y - 1, -tile_rows - 1, rows)
        base = base + (PAD + part * PIECE)

        def blend_rows(read):
            above = read(pl.ds(base, PIECE))
            at = read(pl.ds(base + 1, PIECE))
            return weight_y * above + (1.0 - weight_y) * at

        own = blend_rows(lambda at: planes[tile][at])
        if tile == 1:
            side = jnp.where(rightward, 0, 2)
            beside = blend_rows(lambda at: first[side, at])
        else:
            before, after = planes[(tile - 1) % (tiles + 1)], planes[tile + 1]
            beside = blend_rows(lambda at: jnp.where(rightward, before[at], after[at]))
        at = pltpu.roll(jnp.where(own_at, own, beside), roll_at, 1)
        before = pltpu.roll(jnp.where(own_before, own, beside), roll_before, 1)
        return weight_x * before + (1.0 - weight_x) * at

    parts = tile_rows // PIECE

    def send_piece(slot, dest, tile, part):
        piece = pl.ds(pl.multiple_of(part * PIECE, PIECE), PIECE)
        send[slot, tile, piece] = blend(dest, tile, part)
        pltpu.make_async_remote_copy(
            src_ref=send.at[slot, tile, piece],
            dst_ref=out_ref.at[me, piece, pl.ds(tile * LANES, LANES)],
            send_sem=send_sem,
            recv_sem=recv_sem,
            device_id=(dest, x),
            device_id_type=MESH,
        ).start()

    def send_tile(chips, tile):
        def step(index, carry):
            part, other = index // 2, index % 2
            for chip in chips:
                slot = 2 * CHIPS.index(chip) + other
                send_piece(slot, member(chip, other, 1), tile, part)
            return carry

        lax.fori_loop(0, 2 * parts, step, 0)

    pl.semaphore_wait(barrier, PEERS + 2)

    send_tile(NEAR, 1)
    loads[-1].wait()

    lower = lax.broadcasted_iota(jnp.int32, (64, LANES), 1) < LANES // 2

    def pack(index, carry):
        top = pl.ds(pl.multiple_of(PAD + index * 64, 8), 64)
        bottom = pl.ds(pl.multiple_of(PAD + half + index * 64, 8), 64)
        packed = pl.ds(pl.multiple_of(index * 64, 64), 64)
        low_edge, high_edge = planes[0], planes[tiles - 1]
        pack_out[0, packed] = jnp.where(
            lower, low_edge[top], pltpu.roll(low_edge[bottom], LANES // 2, 1)
        )
        pack_out[1, packed] = jnp.where(
            lower, pltpu.roll(high_edge[bottom], LANES // 2, 1), high_edge[top]
        )
        return carry

    halos = [
        pltpu.make_async_remote_copy(
            src_ref=pack_out.at[side],
            dst_ref=pack_in.at[side],
            send_sem=halo_send_sem.at[side],
            recv_sem=halo_recv_sem.at[side],
            device_id=(me, target),
            device_id_type=MESH,
        )
        for side, target in enumerate((left, right))
    ]

    send_tile(FAR, 1)
    lax.fori_loop(0, half // 64, pack, 0)
    for halo in halos:
        halo.start()

    send_tile(CHIPS, 2)

    for halo in halos:
        halo.wait()

    has_left = x > 0
    has_right = x < 3

    def unpack(index, carry):
        top = pl.ds(pl.multiple_of(PAD + index * 64, 8), 64)
        bottom = pl.ds(pl.multiple_of(PAD + half + index * 64, 8), 64)
        packed = pl.ds(pl.multiple_of(index * 64, 64), 64)
        from_right = jnp.where(has_right, pack_in[0, packed], 0.0)
        from_left = jnp.where(has_left, pack_in[1, packed], 0.0)
        planes[tiles][top] = jnp.where(lower, from_right, from_left)
        planes[tiles][bottom] = pltpu.roll(jnp.where(lower, from_left, from_right), LANES // 2, 1)
        return carry

    lax.fori_loop(0, half // 64, unpack, 0)

    send_tile(CHIPS, 0)
    send_tile(FAR, 3)

    def across(part, carry):
        for tile in range(tiles):
            send_piece(PEERS - 1, member(here, 1, 1), tile, part)
        return carry

    lax.fori_loop(0, parts, across, 0)

    for tile in (3,):
        send_tile(NEAR, tile)

    def keep(part, carry):
        for tile in range(tiles):
            piece = pl.ds(pl.multiple_of(part * PIECE, PIECE), PIECE)
            out_ref[me, piece, pl.ds(tile * LANES, LANES)] = blend(me, tile, part)
        return carry

    lax.fori_loop(0, parts, keep, 0)

    pltpu.make_async_copy(send, send, send_sem).wait()
    pltpu.make_async_copy(send, send, recv_sem).wait()


def body(scenes, offset_y, offset_x, frac_y, frac_x):
    rows, cols = scenes.shape[1:]
    tiles = cols // LANES
    members = lax.axis_size("tm")
    tile_rows = rows // members
    return pl.pallas_call(
        warp_kernel,
        out_shape=jax.ShapeDtypeStruct((members, tile_rows, cols), jnp.float32),
        in_specs=[pl.BlockSpec(memory_space=pltpu.HBM)] * 5,
        out_specs=pl.BlockSpec(memory_space=pltpu.VMEM),
        scratch_shapes=[
            pltpu.SMEM(offset_y.shape, jnp.int32),
            pltpu.SMEM(offset_x.shape, jnp.int32),
            pltpu.SMEM(frac_y.shape, jnp.float32),
            pltpu.SMEM(frac_x.shape, jnp.float32),
            pltpu.VMEM((3, rows + 2 * PAD, LANES), jnp.float32),
            pltpu.VMEM((2, rows + 2 * PAD, LANES), jnp.float32),
            pltpu.VMEM((PEERS, tiles, tile_rows, LANES), jnp.float32),
            pltpu.VMEM((2, rows // 2, LANES), jnp.float32),
            pltpu.VMEM((2, rows // 2, LANES), jnp.float32),
            pltpu.SemaphoreType.DMA((tiles,)),
            pltpu.SemaphoreType.DMA((4,)),
            pltpu.SemaphoreType.DMA(()),
            pltpu.SemaphoreType.DMA(()),
            pltpu.SemaphoreType.DMA((2,)),
            pltpu.SemaphoreType.DMA((2,)),
        ],
        compiler_params=pltpu.CompilerParams(
            collective_id=0, has_side_effects=True, vmem_limit_bytes=28 << 20
        ),
    )(*[pltpu.with_memory_space_constraint(v, pltpu.HBM) for v in (offset_y, offset_x, frac_y, frac_x, scenes)])


def solution(mesh):
    return jax.shard_map(
        body,
        mesh=mesh,
        in_specs=(P("tm", None, "space"), P(), P(), P(), P()),
        out_specs=P(None, "tm", "space"),
        check_vma=False,
    )
```

```python
import jax
import jax.numpy as jnp
from jax import lax
from jax.experimental import pallas as pl
from jax.experimental.pallas import tpu as pltpu
from jax.sharding import PartitionSpec as P

MESH = pl.DeviceIdType.MESH
LANES = 128
PAD = 136
PIECE = 64


NEAR = ((1, 0), (3, 0), (0, 1), (0, 3))
FAR = (
    (2, 2), (2, 1), (1, 2), (2, 3), (3, 2), (2, 0), (0, 2), (1, 1), (3, 3), (1, 3), (3, 1),
)
CHIPS = NEAR + FAR
PEERS = 2 * len(CHIPS) + 1


def warp_kernel(
    oy_hbm, ox_hbm, fy_hbm, fx_hbm, scene_ref, out_ref,
    oy_ref, ox_ref, fy_ref, fx_ref, first, last, send, pack_out, pack_in,
    load_sem, param_sem, send_sem, recv_sem, halo_send_sem, halo_recv_sem, line_sem,
):
    rows = scene_ref.shape[1]
    tiles = scene_ref.shape[2] // LANES
    tile_rows = out_ref.shape[1]
    half = rows // 2
    me = lax.axis_index("tm")
    x = lax.axis_index("space")
    y, z, core = me // 8, (me // 2) % 4, me % 2

    def member(chip, other, sign):
        dy, dz = chip
        return ((y + sign * dy + 4) % 4) * 8 + ((z + sign * dz + 4) % 4) * 2 + (core + other) % 2

    left, right = (x + 3) % 4, (x + 1) % 4
    here = (0, 0)

    planes = [first.at[0], first.at[1], first.at[2], last.at[0], last.at[1]]
    params = ((oy_hbm, oy_ref), (ox_hbm, ox_ref), (fy_hbm, fy_ref), (fx_hbm, fx_ref))
    loads = []
    for index, (hbm, smem) in enumerate(params):
        load = pltpu.make_async_copy(hbm, smem, param_sem.at[index])
        load.start()
        loads.append(load)
    for tile in range(tiles):
        load = pltpu.make_async_copy(
            scene_ref.at[0, :, pl.ds(tile * LANES, LANES)],
            planes[tile].at[pl.ds(PAD, rows)],
            load_sem.at[tile],
        )
        load.start()
        loads.append(load)

    barrier = pltpu.get_barrier_semaphore()
    along_y = tuple((dy, 0) for dy in (2, 1, 3))
    along_z = tuple((0, dz) for dz in (2, 1, 3))
    for chip in along_y + along_z:
        for other in range(2):
            pl.semaphore_signal(
                barrier, inc=1, device_id=(member(chip, other, -1), x), device_id_type=MESH
            )
    pl.semaphore_signal(barrier, inc=1, device_id=(member(here, 1, -1), x), device_id_type=MESH)
    for side in (left, right):
        pl.semaphore_signal(barrier, inc=1, device_id=(me, side), device_id_type=MESH)

    zero_rows = jnp.zeros((PAD, LANES), jnp.float32)
    for plane in planes:
        plane[pl.ds(0, PAD)] = zero_rows
        plane[pl.ds(PAD + rows, PAD)] = zero_rows

    pl.semaphore_wait(barrier, 2 * len(along_y + along_z) + 3)
    for chip in along_z:
        pl.semaphore_signal(
            line_sem, inc=1, device_id=(member(chip, 0, -1), x), device_id_type=MESH
        )
    for load in loads[:-1]:
        load.wait()

    shift_y, shift_x = oy_ref[me], ox_ref[me]
    weight_y, weight_x = fy_ref[me], fx_ref[me]
    lane = lax.broadcasted_iota(jnp.int32, (PIECE, LANES), 1)
    rightward = shift_x >= 0
    low = jnp.where(rightward, 0, -shift_x)
    high = jnp.where(rightward, LANES - shift_x, LANES)
    low_before = jnp.where(rightward, 0, -shift_x - 1)
    high_before = jnp.where(rightward, LANES - 1 - shift_x, LANES)
    own_at = (lane >= low) & (lane < high)
    own_before = (lane >= low_before) & (lane < high_before)
    roll_at = (shift_x + LANES) % LANES
    roll_before = (shift_x + 1 + LANES) % LANES

    def blend(dest, tile, part):
        base = jnp.clip(dest * tile_rows - shift_y - 1, -tile_rows - 1, rows)
        base = base + (PAD + part * PIECE)

        def blend_rows(read):
            above = read(pl.ds(base, PIECE))
            at = read(pl.ds(base + 1, PIECE))
            return weight_y * above + (1.0 - weight_y) * at

        own = blend_rows(lambda at: planes[tile][at])
        if tile == 1:
            side = jnp.where(rightward, 0, 2)
            beside = blend_rows(lambda at: first[side, at])
        else:
            before, after = planes[(tile - 1) % (tiles + 1)], planes[tile + 1]
            beside = blend_rows(lambda at: jnp.where(rightward, before[at], after[at]))
        at = pltpu.roll(jnp.where(own_at, own, beside), roll_at, 1)
        before = pltpu.roll(jnp.where(own_before, own, beside), roll_before, 1)
        return weight_x * before + (1.0 - weight_x) * at

    parts = tile_rows // PIECE

    def send_piece(slot, dest, tile, part):
        piece = pl.ds(pl.multiple_of(part * PIECE, PIECE), PIECE)
        send[slot, tile, piece] = blend(dest, tile, part)
        pltpu.make_async_remote_copy(
            src_ref=send.at[slot, tile, piece],
            dst_ref=out_ref.at[me, piece, pl.ds(tile * LANES, LANES)],
            send_sem=send_sem,
            recv_sem=recv_sem,
            device_id=(dest, x),
            device_id_type=MESH,
        ).start()

    def send_tile(chips, tile):
        def step(index, carry):
            part, other = index // 2, index % 2
            for chip in chips:
                slot = 2 * CHIPS.index(chip) + other
                send_piece(slot, member(chip, other, 1), tile, part)
            return carry

        lax.fori_loop(0, 2 * parts, step, 0)

    send_tile(NEAR, 1)
    pl.semaphore_wait(line_sem, len(along_z))
    loads[-1].wait()

    lower = lax.broadcasted_iota(jnp.int32, (64, LANES), 1) < LANES // 2

    def pack(index, carry):
        top = pl.ds(pl.multiple_of(PAD + index * 64, 8), 64)
        bottom = pl.ds(pl.multiple_of(PAD + half + index * 64, 8), 64)
        packed = pl.ds(pl.multiple_of(index * 64, 64), 64)
        low_edge, high_edge = planes[0], planes[tiles - 1]
        pack_out[0, packed] = jnp.where(
            lower, low_edge[top], pltpu.roll(low_edge[bottom], LANES // 2, 1)
        )
        pack_out[1, packed] = jnp.where(
            lower, pltpu.roll(high_edge[bottom], LANES // 2, 1), high_edge[top]
        )
        return carry

    halos = [
        pltpu.make_async_remote_copy(
            src_ref=pack_out.at[side],
            dst_ref=pack_in.at[side],
            send_sem=halo_send_sem.at[side],
            recv_sem=halo_recv_sem.at[side],
            device_id=(me, target),
            device_id_type=MESH,
        )
        for side, target in enumerate((left, right))
    ]

    send_tile(FAR, 1)
    send_tile(CHIPS, 2)
    lax.fori_loop(0, half // 64, pack, 0)
    for halo in halos:
        halo.start()

    for halo in halos:
        halo.wait()

    has_left = x > 0
    has_right = x < 3

    def unpack(index, carry):
        top = pl.ds(pl.multiple_of(PAD + index * 64, 8), 64)
        bottom = pl.ds(pl.multiple_of(PAD + half + index * 64, 8), 64)
        packed = pl.ds(pl.multiple_of(index * 64, 64), 64)
        from_right = jnp.where(has_right, pack_in[0, packed], 0.0)
        from_left = jnp.where(has_left, pack_in[1, packed], 0.0)
        planes[tiles][top] = jnp.where(lower, from_right, from_left)
        planes[tiles][bottom] = pltpu.roll(jnp.where(lower, from_left, from_right), LANES // 2, 1)
        return carry

    lax.fori_loop(0, half // 64, unpack, 0)

    send_tile(CHIPS, 0)
    send_tile(FAR, 3)

    def across(part, carry):
        for tile in range(tiles):
            send_piece(PEERS - 1, member(here, 1, 1), tile, part)
        return carry

    lax.fori_loop(0, parts, across, 0)

    for tile in (3,):
        send_tile(NEAR, tile)

    def keep(part, carry):
        for tile in range(tiles):
            piece = pl.ds(pl.multiple_of(part * PIECE, PIECE), PIECE)
            out_ref[me, piece, pl.ds(tile * LANES, LANES)] = blend(me, tile, part)
        return carry

    lax.fori_loop(0, parts, keep, 0)

    pltpu.make_async_copy(send, send, send_sem).wait()
    pltpu.make_async_copy(send, send, recv_sem).wait()


def body(scenes, offset_y, offset_x, frac_y, frac_x):
    rows, cols = scenes.shape[1:]
    tiles = cols // LANES
    members = lax.axis_size("tm")
    tile_rows = rows // members
    return pl.pallas_call(
        warp_kernel,
        out_shape=jax.ShapeDtypeStruct((members, tile_rows, cols), jnp.float32),
        in_specs=[pl.BlockSpec(memory_space=pltpu.HBM)] * 5,
        out_specs=pl.BlockSpec(memory_space=pltpu.VMEM),
        scratch_shapes=[
            pltpu.SMEM(offset_y.shape, jnp.int32),
            pltpu.SMEM(offset_x.shape, jnp.int32),
            pltpu.SMEM(frac_y.shape, jnp.float32),
            pltpu.SMEM(frac_x.shape, jnp.float32),
            pltpu.VMEM((3, rows + 2 * PAD, LANES), jnp.float32),
            pltpu.VMEM((2, rows + 2 * PAD, LANES), jnp.float32),
            pltpu.VMEM((PEERS, tiles, tile_rows, LANES), jnp.float32),
            pltpu.VMEM((2, rows // 2, LANES), jnp.float32),
            pltpu.VMEM((2, rows // 2, LANES), jnp.float32),
            pltpu.SemaphoreType.DMA((tiles,)),
            pltpu.SemaphoreType.DMA((4,)),
            pltpu.SemaphoreType.DMA(()),
            pltpu.SemaphoreType.DMA(()),
            pltpu.SemaphoreType.DMA((2,)),
            pltpu.SemaphoreType.DMA((2,)),
            pltpu.SemaphoreType.REGULAR,
        ],
        compiler_params=pltpu.CompilerParams(
            collective_id=0, has_side_effects=True, vmem_limit_bytes=28 << 20
        ),
    )(*[pltpu.with_memory_space_constraint(v, pltpu.HBM) for v in (offset_y, offset_x, frac_y, frac_x, scenes)])


def solution(mesh):
    return jax.shard_map(
        body,
        mesh=mesh,
        in_specs=(P("tm", None, "space"), P(), P(), P(), P()),
        out_specs=P(None, "tm", "space"),
        check_vma=False,
    )
```

```python
import jax
import jax.numpy as jnp
from jax import lax
from jax.experimental import pallas as pl
from jax.experimental.pallas import tpu as pltpu
from jax.sharding import PartitionSpec as P

MESH = pl.DeviceIdType.MESH
LANES = 128
PAD = 136
PIECE = 64


NEAR = ((1, 0), (3, 0), (0, 1), (0, 3))
FAR = (
    (2, 2), (2, 1), (1, 2), (2, 3), (3, 2), (2, 0), (0, 2), (1, 1), (3, 3), (1, 3), (3, 1),
)
CHIPS = NEAR + FAR
PEERS = 2 * len(CHIPS) + 1


def warp_kernel(
    oy_hbm, ox_hbm, fy_hbm, fx_hbm, scene_ref, out_ref,
    oy_ref, ox_ref, fy_ref, fx_ref, first, last, send, pack_out, pack_in,
    load_sem, param_sem, send_sem, recv_sem, halo_send_sem, halo_recv_sem, line_sem,
):
    rows = scene_ref.shape[1]
    tiles = scene_ref.shape[2] // LANES
    tile_rows = out_ref.shape[1]
    half = rows // 2
    me = lax.axis_index("tm")
    x = lax.axis_index("space")
    y, z, core = me // 8, (me // 2) % 4, me % 2

    def member(chip, other, sign):
        dy, dz = chip
        return ((y + sign * dy + 4) % 4) * 8 + ((z + sign * dz + 4) % 4) * 2 + (core + other) % 2

    left, right = (x + 3) % 4, (x + 1) % 4
    here = (0, 0)

    planes = [first.at[0], first.at[1], first.at[2], last.at[0], last.at[1]]
    params = ((oy_hbm, oy_ref), (ox_hbm, ox_ref), (fy_hbm, fy_ref), (fx_hbm, fx_ref))
    loads = []
    for index, (hbm, smem) in enumerate(params):
        load = pltpu.make_async_copy(hbm, smem, param_sem.at[index])
        load.start()
        loads.append(load)
    for tile in range(tiles):
        load = pltpu.make_async_copy(
            scene_ref.at[0, :, pl.ds(tile * LANES, LANES)],
            planes[tile].at[pl.ds(PAD, rows)],
            load_sem.at[tile],
        )
        load.start()
        loads.append(load)

    barrier = pltpu.get_barrier_semaphore()
    along_y = tuple((dy, 0) for dy in (2, 1, 3))
    along_z = tuple((0, dz) for dz in (2, 1, 3))
    for chip in along_y + along_z:
        for other in range(2):
            pl.semaphore_signal(
                barrier, inc=1, device_id=(member(chip, other, -1), x), device_id_type=MESH
            )
    pl.semaphore_signal(barrier, inc=1, device_id=(member(here, 1, -1), x), device_id_type=MESH)
    for side in (left, right):
        pl.semaphore_signal(barrier, inc=1, device_id=(me, side), device_id_type=MESH)

    zero_rows = jnp.zeros((PAD, LANES), jnp.float32)
    for plane in planes:
        plane[pl.ds(0, PAD)] = zero_rows
        plane[pl.ds(PAD + rows, PAD)] = zero_rows

    pl.semaphore_wait(barrier, 2 * len(along_y + along_z) + 3)
    for chip in along_z:
        pl.semaphore_signal(
            line_sem, inc=1, device_id=(member(chip, 0, -1), x), device_id_type=MESH
        )
    for load in loads[:-1]:
        load.wait()

    shift_y, shift_x = oy_ref[me], ox_ref[me]
    weight_y, weight_x = fy_ref[me], fx_ref[me]
    lane = lax.broadcasted_iota(jnp.int32, (PIECE, LANES), 1)
    rightward = shift_x >= 0
    low = jnp.where(rightward, 0, -shift_x)
    high = jnp.where(rightward, LANES - shift_x, LANES)
    low_before = jnp.where(rightward, 0, -shift_x - 1)
    high_before = jnp.where(rightward, LANES - 1 - shift_x, LANES)
    own_at = (lane >= low) & (lane < high)
    own_before = (lane >= low_before) & (lane < high_before)
    roll_at = (shift_x + LANES) % LANES
    roll_before = (shift_x + 1 + LANES) % LANES

    def blend(dest, tile, part):
        base = jnp.clip(dest * tile_rows - shift_y - 1, -tile_rows - 1, rows)
        base = base + (PAD + part * PIECE)

        def blend_rows(read):
            above = read(pl.ds(base, PIECE))
            at = read(pl.ds(base + 1, PIECE))
            return weight_y * above + (1.0 - weight_y) * at

        own = blend_rows(lambda at: planes[tile][at])
        if tile == 1:
            side = jnp.where(rightward, 0, 2)
            beside = blend_rows(lambda at: first[side, at])
        else:
            before, after = planes[(tile - 1) % (tiles + 1)], planes[tile + 1]
            beside = blend_rows(lambda at: jnp.where(rightward, before[at], after[at]))
        at = pltpu.roll(jnp.where(own_at, own, beside), roll_at, 1)
        before = pltpu.roll(jnp.where(own_before, own, beside), roll_before, 1)
        return weight_x * before + (1.0 - weight_x) * at

    parts = tile_rows // PIECE

    def send_piece(slot, dest, tile, part):
        piece = pl.ds(pl.multiple_of(part * PIECE, PIECE), PIECE)
        send[slot, tile, piece] = blend(dest, tile, part)
        pltpu.make_async_remote_copy(
            src_ref=send.at[slot, tile, piece],
            dst_ref=out_ref.at[me, piece, pl.ds(tile * LANES, LANES)],
            send_sem=send_sem,
            recv_sem=recv_sem,
            device_id=(dest, x),
            device_id_type=MESH,
        ).start()

    def send_tile(chips, tile):
        def step(index, carry):
            part, other = index % parts, (index // parts + core) % 2
            for chip in chips:
                slot = 2 * CHIPS.index(chip) + other
                send_piece(slot, member(chip, other, 1), tile, part)
            return carry

        lax.fori_loop(0, 2 * parts, step, 0)

    send_tile(NEAR, 1)
    pl.semaphore_wait(line_sem, len(along_z))
    loads[-1].wait()

    lower = lax.broadcasted_iota(jnp.int32, (64, LANES), 1) < LANES // 2

    def pack(index, carry):
        top = pl.ds(pl.multiple_of(PAD + index * 64, 8), 64)
        bottom = pl.ds(pl.multiple_of(PAD + half + index * 64, 8), 64)
        packed = pl.ds(pl.multiple_of(index * 64, 64), 64)
        low_edge, high_edge = planes[0], planes[tiles - 1]
        pack_out[0, packed] = jnp.where(
            lower, low_edge[top], pltpu.roll(low_edge[bottom], LANES // 2, 1)
        )
        pack_out[1, packed] = jnp.where(
            lower, pltpu.roll(high_edge[bottom], LANES // 2, 1), high_edge[top]
        )
        return carry

    halos = [
        pltpu.make_async_remote_copy(
            src_ref=pack_out.at[side],
            dst_ref=pack_in.at[side],
            send_sem=halo_send_sem.at[side],
            recv_sem=halo_recv_sem.at[side],
            device_id=(me, target),
            device_id_type=MESH,
        )
        for side, target in enumerate((left, right))
    ]

    send_tile(FAR, 1)
    send_tile(CHIPS, 2)
    lax.fori_loop(0, half // 64, pack, 0)
    for halo in halos:
        halo.start()

    for halo in halos:
        halo.wait()

    has_left = x > 0
    has_right = x < 3

    def unpack(index, carry):
        top = pl.ds(pl.multiple_of(PAD + index * 64, 8), 64)
        bottom = pl.ds(pl.multiple_of(PAD + half + index * 64, 8), 64)
        packed = pl.ds(pl.multiple_of(index * 64, 64), 64)
        from_right = jnp.where(has_right, pack_in[0, packed], 0.0)
        from_left = jnp.where(has_left, pack_in[1, packed], 0.0)
        planes[tiles][top] = jnp.where(lower, from_right, from_left)
        planes[tiles][bottom] = pltpu.roll(jnp.where(lower, from_left, from_right), LANES // 2, 1)
        return carry

    lax.fori_loop(0, half // 64, unpack, 0)

    send_tile(CHIPS, 0)
    send_tile(FAR, 3)

    def across(part, carry):
        for tile in range(tiles):
            send_piece(PEERS - 1, member(here, 1, 1), tile, part)
        return carry

    lax.fori_loop(0, parts, across, 0)

    for tile in (3,):
        send_tile(NEAR, tile)

    def keep(part, carry):
        for tile in range(tiles):
            piece = pl.ds(pl.multiple_of(part * PIECE, PIECE), PIECE)
            out_ref[me, piece, pl.ds(tile * LANES, LANES)] = blend(me, tile, part)
        return carry

    lax.fori_loop(0, parts, keep, 0)

    pltpu.make_async_copy(send, send, send_sem).wait()
    pltpu.make_async_copy(send, send, recv_sem).wait()


def body(scenes, offset_y, offset_x, frac_y, frac_x):
    rows, cols = scenes.shape[1:]
    tiles = cols // LANES
    members = lax.axis_size("tm")
    tile_rows = rows // members
    return pl.pallas_call(
        warp_kernel,
        out_shape=jax.ShapeDtypeStruct((members, tile_rows, cols), jnp.float32),
        in_specs=[pl.BlockSpec(memory_space=pltpu.HBM)] * 5,
        out_specs=pl.BlockSpec(memory_space=pltpu.VMEM),
        scratch_shapes=[
            pltpu.SMEM(offset_y.shape, jnp.int32),
            pltpu.SMEM(offset_x.shape, jnp.int32),
            pltpu.SMEM(frac_y.shape, jnp.float32),
            pltpu.SMEM(frac_x.shape, jnp.float32),
            pltpu.VMEM((3, rows + 2 * PAD, LANES), jnp.float32),
            pltpu.VMEM((2, rows + 2 * PAD, LANES), jnp.float32),
            pltpu.VMEM((PEERS, tiles, tile_rows, LANES), jnp.float32),
            pltpu.VMEM((2, rows // 2, LANES), jnp.float32),
            pltpu.VMEM((2, rows // 2, LANES), jnp.float32),
            pltpu.SemaphoreType.DMA((tiles,)),
            pltpu.SemaphoreType.DMA((4,)),
            pltpu.SemaphoreType.DMA(()),
            pltpu.SemaphoreType.DMA(()),
            pltpu.SemaphoreType.DMA((2,)),
            pltpu.SemaphoreType.DMA((2,)),
            pltpu.SemaphoreType.REGULAR,
        ],
        compiler_params=pltpu.CompilerParams(
            collective_id=0, has_side_effects=True, vmem_limit_bytes=36 << 20
        ),
    )(*[pltpu.with_memory_space_constraint(v, pltpu.HBM) for v in (offset_y, offset_x, frac_y, frac_x, scenes)])


def solution(mesh):
    return jax.shard_map(
        body,
        mesh=mesh,
        in_specs=(P("tm", None, "space"), P(), P(), P(), P()),
        out_specs=P(None, "tm", "space"),
        check_vma=False,
    )
```

```python
import jax
import jax.numpy as jnp
from jax import lax
from jax.experimental import pallas as pl
from jax.experimental.pallas import tpu as pltpu
from jax.sharding import PartitionSpec as P

MESH = pl.DeviceIdType.MESH
LANES = 128
PAD = 136
PIECE = 64
HEAD = 128


NEAR = ((1, 0), (3, 0), (0, 1), (0, 3))
FAR = (
    (2, 2), (2, 1), (1, 2), (2, 3), (3, 2), (2, 0), (0, 2), (1, 1), (3, 3), (1, 3), (3, 1),
)
CHIPS = NEAR + FAR
PEERS = 2 * len(CHIPS) + 1


def warp_kernel(
    oy_hbm, ox_hbm, fy_hbm, fx_hbm, scene_ref, out_ref,
    oy_ref, ox_ref, fy_ref, fx_ref, first, last, send, pack_out, pack_in,
    load_sem, param_sem, send_sem, recv_sem, halo_send_sem, halo_recv_sem, line_sem,
):
    rows = scene_ref.shape[1]
    tiles = scene_ref.shape[2] // LANES
    tile_rows = out_ref.shape[1]
    half = rows // 2
    me = lax.axis_index("tm")
    x = lax.axis_index("space")
    y, z, core = me // 8, (me // 2) % 4, me % 2

    def member(chip, other, sign):
        dy, dz = chip
        return ((y + sign * dy + 4) % 4) * 8 + ((z + sign * dz + 4) % 4) * 2 + (core + other) % 2

    left, right = (x + 3) % 4, (x + 1) % 4
    here = (0, 0)

    planes = [first.at[0], first.at[1], first.at[2], last.at[0], last.at[1]]
    params = ((oy_hbm, oy_ref), (ox_hbm, ox_ref), (fy_hbm, fy_ref), (fx_hbm, fx_ref))
    loads = []
    for index, (hbm, smem) in enumerate(params):
        load = pltpu.make_async_copy(hbm, smem, param_sem.at[index])
        load.start()
        loads.append(load)
    for tile in range(tiles):
        load = pltpu.make_async_copy(
            scene_ref.at[0, :, pl.ds(tile * LANES, LANES)],
            planes[tile].at[pl.ds(PAD, rows)],
            load_sem.at[tile],
        )
        load.start()
        loads.append(load)

    barrier = pltpu.get_barrier_semaphore()
    along_y = tuple((dy, 0) for dy in (2, 1, 3))
    along_z = tuple((0, dz) for dz in (2, 1, 3))
    for chip in along_y + along_z:
        for other in range(2):
            pl.semaphore_signal(
                barrier, inc=1, device_id=(member(chip, other, -1), x), device_id_type=MESH
            )
    pl.semaphore_signal(barrier, inc=1, device_id=(member(here, 1, -1), x), device_id_type=MESH)
    for side in (left, right):
        pl.semaphore_signal(barrier, inc=1, device_id=(me, side), device_id_type=MESH)

    zero_rows = jnp.zeros((PAD, LANES), jnp.float32)
    for plane in planes:
        plane[pl.ds(0, PAD)] = zero_rows
        plane[pl.ds(PAD + rows, PAD)] = zero_rows

    pl.semaphore_wait(barrier, 2 * len(along_y + along_z) + 3)
    for chip in along_z:
        pl.semaphore_signal(
            line_sem, inc=1, device_id=(member(chip, 0, -1), x), device_id_type=MESH
        )
    for load in loads[:-1]:
        load.wait()

    shift_y, shift_x = oy_ref[me], ox_ref[me]
    weight_y, weight_x = fy_ref[me], fx_ref[me]
    lane = lax.broadcasted_iota(jnp.int32, (1, LANES), 1)
    rightward = shift_x >= 0
    low = jnp.where(rightward, 0, -shift_x)
    high = jnp.where(rightward, LANES - shift_x, LANES)
    low_before = jnp.where(rightward, 0, -shift_x - 1)
    high_before = jnp.where(rightward, LANES - 1 - shift_x, LANES)
    own_at = (lane >= low) & (lane < high)
    own_before = (lane >= low_before) & (lane < high_before)
    roll_at = (shift_x + LANES) % LANES
    roll_before = (shift_x + 1 + LANES) % LANES

    def blend(dest, tile, part, size=PIECE):
        base = jnp.clip(dest * tile_rows - shift_y - 1, -tile_rows - 1, rows)
        base = base + (PAD + part * size)

        def blend_rows(read):
            above = read(pl.ds(base, size))
            at = read(pl.ds(base + 1, size))
            return weight_y * above + (1.0 - weight_y) * at

        own = blend_rows(lambda at: planes[tile][at])
        if tile == 1:
            side = jnp.where(rightward, 0, 2)
            beside = blend_rows(lambda at: first[side, at])
        else:
            before, after = planes[(tile - 1) % (tiles + 1)], planes[tile + 1]
            beside = blend_rows(lambda at: jnp.where(rightward, before[at], after[at]))
        at = pltpu.roll(jnp.where(jnp.broadcast_to(own_at, own.shape), own, beside), roll_at, 1)
        before = pltpu.roll(jnp.where(jnp.broadcast_to(own_before, own.shape), own, beside), roll_before, 1)
        return weight_x * before + (1.0 - weight_x) * at

    parts = tile_rows // PIECE

    def send_piece(slot, dest, tile, part, size=PIECE):
        piece = pl.ds(pl.multiple_of(part * size, size), size)
        send[slot, tile, piece] = blend(dest, tile, part, size)
        pltpu.make_async_remote_copy(
            src_ref=send.at[slot, tile, piece],
            dst_ref=out_ref.at[me, piece, pl.ds(tile * LANES, LANES)],
            send_sem=send_sem,
            recv_sem=recv_sem,
            device_id=(dest, x),
            device_id_type=MESH,
        ).start()

    def send_tile(chips, tile, size=PIECE):
        parts = tile_rows // size

        def step(index, carry):
            part, other = index % parts, (index // parts + core) % 2
            for chip in chips:
                slot = 2 * CHIPS.index(chip) + other
                send_piece(slot, member(chip, other, 1), tile, part, size)
            return carry

        lax.fori_loop(0, 2 * parts, step, 0)

    send_tile(NEAR, 1, HEAD)
    pl.semaphore_wait(line_sem, len(along_z))
    loads[-1].wait()

    lower = lax.broadcasted_iota(jnp.int32, (64, LANES), 1) < LANES // 2

    def pack(index, carry):
        top = pl.ds(pl.multiple_of(PAD + index * 64, 8), 64)
        bottom = pl.ds(pl.multiple_of(PAD + half + index * 64, 8), 64)
        packed = pl.ds(pl.multiple_of(index * 64, 64), 64)
        low_edge, high_edge = planes[0], planes[tiles - 1]
        pack_out[0, packed] = jnp.where(
            lower, low_edge[top], pltpu.roll(low_edge[bottom], LANES // 2, 1)
        )
        pack_out[1, packed] = jnp.where(
            lower, pltpu.roll(high_edge[bottom], LANES // 2, 1), high_edge[top]
        )
        return carry

    halos = [
        pltpu.make_async_remote_copy(
            src_ref=pack_out.at[side],
            dst_ref=pack_in.at[side],
            send_sem=halo_send_sem.at[side],
            recv_sem=halo_recv_sem.at[side],
            device_id=(me, target),
            device_id_type=MESH,
        )
        for side, target in enumerate((left, right))
    ]

    send_tile(FAR, 1)
    send_tile(CHIPS, 2)
    lax.fori_loop(0, half // 64, pack, 0)
    for halo in halos:
        halo.start()

    for halo in halos:
        halo.wait()

    has_left = x > 0
    has_right = x < 3

    def unpack(index, carry):
        top = pl.ds(pl.multiple_of(PAD + index * 64, 8), 64)
        bottom = pl.ds(pl.multiple_of(PAD + half + index * 64, 8), 64)
        packed = pl.ds(pl.multiple_of(index * 64, 64), 64)
        from_right = jnp.where(has_right, pack_in[0, packed], 0.0)
        from_left = jnp.where(has_left, pack_in[1, packed], 0.0)
        planes[tiles][top] = jnp.where(lower, from_right, from_left)
        planes[tiles][bottom] = pltpu.roll(jnp.where(lower, from_left, from_right), LANES // 2, 1)
        return carry

    lax.fori_loop(0, half // 64, unpack, 0)

    send_tile(CHIPS, 0)
    send_tile(FAR, 3)

    def across(part, carry):
        for tile in range(tiles):
            send_piece(PEERS - 1, member(here, 1, 1), tile, part)
        return carry

    lax.fori_loop(0, parts, across, 0)

    for tile in (3,):
        send_tile(NEAR, tile)

    def keep(part, carry):
        for tile in range(tiles):
            piece = pl.ds(pl.multiple_of(part * PIECE, PIECE), PIECE)
            out_ref[me, piece, pl.ds(tile * LANES, LANES)] = blend(me, tile, part)
        return carry

    lax.fori_loop(0, parts, keep, 0)

    pltpu.make_async_copy(send, send, send_sem).wait()
    pltpu.make_async_copy(send, send, recv_sem).wait()


def body(scenes, offset_y, offset_x, frac_y, frac_x):
    rows, cols = scenes.shape[1:]
    tiles = cols // LANES
    members = lax.axis_size("tm")
    tile_rows = rows // members
    return pl.pallas_call(
        warp_kernel,
        out_shape=jax.ShapeDtypeStruct((members, tile_rows, cols), jnp.float32),
        in_specs=[pl.BlockSpec(memory_space=pltpu.HBM)] * 5,
        out_specs=pl.BlockSpec(memory_space=pltpu.VMEM),
        scratch_shapes=[
            pltpu.SMEM(offset_y.shape, jnp.int32),
            pltpu.SMEM(offset_x.shape, jnp.int32),
            pltpu.SMEM(frac_y.shape, jnp.float32),
            pltpu.SMEM(frac_x.shape, jnp.float32),
            pltpu.VMEM((3, rows + 2 * PAD, LANES), jnp.float32),
            pltpu.VMEM((2, rows + 2 * PAD, LANES), jnp.float32),
            pltpu.VMEM((PEERS, tiles, tile_rows, LANES), jnp.float32),
            pltpu.VMEM((2, rows // 2, LANES), jnp.float32),
            pltpu.VMEM((2, rows // 2, LANES), jnp.float32),
            pltpu.SemaphoreType.DMA((tiles,)),
            pltpu.SemaphoreType.DMA((4,)),
            pltpu.SemaphoreType.DMA(()),
            pltpu.SemaphoreType.DMA(()),
            pltpu.SemaphoreType.DMA((2,)),
            pltpu.SemaphoreType.DMA((2,)),
            pltpu.SemaphoreType.REGULAR,
        ],
        compiler_params=pltpu.CompilerParams(
            collective_id=0, has_side_effects=True, vmem_limit_bytes=36 << 20
        ),
    )(*[pltpu.with_memory_space_constraint(v, pltpu.HBM) for v in (offset_y, offset_x, frac_y, frac_x, scenes)])


def solution(mesh):
    return jax.shard_map(
        body,
        mesh=mesh,
        in_specs=(P("tm", None, "space"), P(), P(), P(), P()),
        out_specs=P(None, "tm", "space"),
        check_vma=False,
    )
```
